32 devices in a mesh: pt: 8 (over z, y), tm: 4 (over x, core).
Axes of the slice: x: 2, y: 2, z: 4, core: 2. Of those that a mesh axis runs over, the one named last changes fastest.
Arguments:
- signals: float32 [512, 32768], P('pt', 'tm'), may hold values from -6 to 6
- freq_bins: int32 [4], replicated, may hold values from 1 to 511
Outputs:
- cross_spectra: float32 [2, 4, 512, 512], P(None, None, 'pt', 'tm')
The draws below stay inside these ranges and needn't reach their ends.
All inputs are finite; a program needn't handle non-finite values.
Results may differ from the reference program's by a relative error of at most 0.000064.
Values sent between devices are 32-bit elements; how exact they have to be, the bound alone decides.
No kernel may reach another device: no remote copies, remote signals or barrier semaphores. Data moves between devices by JAX's collectives and lax.ppermute only.
A program may use at most 64 MiB of HBM per device.

```python
import math
import jax
import jax.numpy as jnp
from jax import lax

SEGLEN = 1024
NFREQ = 4
HOP = 512
TIME = 32768
POINTS = 512
NSEG = 63


def set_ends(result, key, least, high):
    longest = result.shape.index(max(result.shape))
    spots = []
    for shift in (0, 1):
        where = [jax.random.randint(jax.random.fold_in(key, axis), (), 0, length) for axis, length in enumerate(result.shape)]
        where[longest] = (where[longest] + shift) % result.shape[longest]
        spots.append(tuple(where))
    return result.at[spots[0]].set(least).at[spots[1]].set(high)


def steps_of(key, dims, split, low, high):
    factor_of = 1.0
    for position, shards_of in split:
        steps = jax.random.uniform(jax.random.fold_in(jax.random.fold_in(key, 6), position), (shards_of,), jnp.float32, low / len(split), high / len(split))
        factor_of = factor_of * jnp.repeat(jnp.exp(steps), dims[position] // shards_of).reshape((-1,) + (1,) * (len(dims) - 1 - position))
    return factor_of


def gaussian(key, dims, scale, limit, pieces=(), kind=jnp.bfloat16):
    entries = scale * jax.random.normal(key, dims, jnp.float32)
    if pieces:
        entries = entries * steps_of(key, dims, pieces, -0.22, 0.18)
    return jnp.clip(entries, -limit, limit).astype(kind)


def setup_inputs(seed: int = 0) -> dict:
    keys = jax.random.split(jax.random.key(seed), 3)
    signals = gaussian(keys[0], (POINTS, TIME), 1.0, 6.0, ((0, 8), (1, 4)), jnp.float32)
    freq_bins = set_ends(jax.random.randint(keys[1], (NFREQ,), 1, HOP), jax.random.fold_in(keys[1], 1), 1, HOP - 1).astype(jnp.int32)
    return dict(signals=signals, freq_bins=freq_bins)


TWO_PI = 2.0 * math.pi


def dft_tables(freq_bins, seg_len):
    sample_index = jnp.arange(seg_len, dtype=jnp.int32)
    wrapped = (sample_index[:, None] * freq_bins[None, :].astype(jnp.int32)) % seg_len
    angles = wrapped.astype(jnp.float32) * (TWO_PI / seg_len)
    window = 0.5 - 0.5 * jnp.cos(sample_index.astype(jnp.float32) * (TWO_PI / seg_len))
    cosine = window[:, None] * jnp.cos(angles)
    sine_part = -window[:, None] * jnp.sin(angles)
    full_table = jnp.concatenate([cosine, sine_part], axis=1)
    half_len = seg_len // 2
    return jnp.concatenate([full_table[:half_len], full_table[half_len:]], axis=1)


def tile_products(left_side, right_side):
    stacked_right = jnp.concatenate([right_side[:, 0], right_side[:, 1]], axis=2)
    real_left = jnp.concatenate([left_side[:, 0], left_side[:, 1]], axis=2)
    imag_left = jnp.concatenate([left_side[:, 1], -left_side[:, 0]], axis=2)
    real_part = jnp.einsum("fps,fqs->fpq", real_left, stacked_right, precision=lax.Precision.HIGHEST)
    imag_part = jnp.einsum("fps,fqs->fpq", imag_left, stacked_right, precision=lax.Precision.HIGHEST)
    return jnp.stack([real_part, imag_part])


def reference(signals, freq_bins):
    table = dft_tables(freq_bins, SEGLEN)
    half_len = SEGLEN // 2
    columns = 2 * NFREQ
    blocks = signals.reshape(POINTS, TIME // half_len, half_len)
    projected = jnp.einsum("pbn,nc->pbc", blocks, table, precision=lax.Precision.HIGHEST)
    spectra = projected[:, :-1, :columns] + projected[:, 1:, columns:]
    spectra_panel = spectra.reshape(POINTS, NSEG, 2, NFREQ).transpose(3, 2, 0, 1)
    scale = 1.0 / (NSEG * 0.375 * SEGLEN)
    return tile_products(spectra_panel, spectra_panel) * scale
```

```python
import functools
import math

import jax
import jax.numpy as jnp
from jax import lax
from jax.experimental import pallas as pl
from jax.experimental.pallas import tpu as pltpu
from jax.sharding import PartitionSpec as P

SEGLEN = 1024
HALF = SEGLEN // 2
NFREQ = 4
COLS = 2 * NFREQ
LANES = 128
SERIES = [(-1) ** n / math.factorial(2 * n) for n in range(8)]
CONTRACT_LAST = (((1,), (1,)), ((), ()))
CONTRACT_FIRST = (((0,), (0,)), ((), ()))


def cosine_of(steps):
    wrapped = ((steps + HALF) & (SEGLEN - 1)) - HALF
    size = jnp.abs(wrapped)
    folded = size > HALF // 2
    size = jnp.where(folded, HALF - size, size)
    angle = size.astype(jnp.float32) * (2.0 * math.pi / SEGLEN)
    square = angle * angle
    value = jnp.full_like(square, SERIES[-1])
    for term in SERIES[-2::-1]:
        value = value * square + term
    return jnp.where(folded, -value, value)


def split(value):
    high = value.astype(jnp.bfloat16)
    low = (value - high.astype(jnp.float32)).astype(jnp.bfloat16)
    return high, low


def project_kernel(bins_ref, signals_ref, out_ref, held, sems):
    pairs, width, _ = held.shape
    points = width // 2
    copies = []
    for j in range(pairs):
        for h in range(2):
            copies.append(
                pltpu.make_async_copy(
                    signals_ref.at[:, pl.ds((j + pairs * h) * HALF, HALF)],
                    held.at[j, pl.ds(h * points, points), :],
                    sems.at[j, h],
                )
            )
            copies[-1].start()
    row = lax.broadcasted_iota(jnp.int32, (COLS, SEGLEN), 0)
    sample = lax.broadcasted_iota(jnp.int32, (COLS, SEGLEN), 1)
    bins = jnp.zeros((COLS, SEGLEN), jnp.int32)
    for f in range(NFREQ):
        bins = jnp.where(row % NFREQ == f, bins_ref[f], bins)
    window = 0.5 - 0.5 * cosine_of(sample)
    quarter = jnp.where(row >= NFREQ, SEGLEN // 4, 0)
    table = window * cosine_of(sample * bins + quarter)
    high, low = split(jnp.concatenate([table[:, :HALF], table[:, HALF:]], axis=0))
    both = jnp.concatenate([high, low], axis=0)
    first, second = [], []
    step = 4 if pairs % 4 == 0 else 1
    for j in range(0, pairs, step):
        for copy in copies[2 * j : 2 * (j + step)]:
            copy.wait()
        block = jnp.concatenate([held[j + q] for q in range(step)], axis=0)
        block_high, block_low = split(block)
        main = lax.dot_general(both, block_high, CONTRACT_LAST, preferred_element_type=jnp.float32)
        rest = lax.dot_general(high, block_low, CONTRACT_LAST, preferred_element_type=jnp.float32)
        sums = main[: 2 * COLS] + main[2 * COLS :] + rest
        for q in range(step):
            first.append(sums[:COLS, q * width : (q + 1) * width])
            second.append(sums[COLS:, q * width : (q + 1) * width])
    for j in range(pairs - 1):
        out_ref[j * COLS : (j + 1) * COLS, :] = first[j] + second[j + 1]
    lane = lax.broadcasted_iota(jnp.int32, (COLS, width), 1)
    wrap = jnp.where(lane < points, pltpu.roll(second[0], points, 1), 0.0)
    out_ref[(pairs - 1) * COLS : pairs * COLS, :] = first[pairs - 1] + wrap
    out_ref[pairs * COLS :, :] = second[0]


def project(signals, freq_bins):
    points, samples = signals.shape
    pairs = samples // HALF // 2
    return pl.pallas_call(
        project_kernel,
        out_shape=jax.ShapeDtypeStruct(((pairs + 1) * COLS, 2 * points), jnp.float32),
        in_specs=[pl.BlockSpec(memory_space=pltpu.SMEM), pl.BlockSpec(memory_space=pl.ANY)],
        out_specs=pl.BlockSpec(memory_space=pltpu.VMEM),
        scratch_shapes=[
            pltpu.VMEM((pairs, 2 * points, HALF), jnp.float32),
            pltpu.SemaphoreType.DMA((pairs, 2)),
        ],
        name="project",
    )(freq_bins, signals)


def tiles_kernel(chips, ratio, scale, place_ref, *refs):
    own_ref = refs[0]
    row_refs = refs[1:chips]
    column_refs = refs[chips : chips + chips * ratio]
    out_ref, left, right = refs[chips + chips * ratio :]
    chip, target, sub = place_ref[0], place_ref[1], place_ref[2]
    rows = left.shape[2]
    pairs = rows // COLS - 1
    points = LANES // 2

    def put(dst, src):
        for c in range(2):
            dst[c] = src[c * rows : (c + 1) * rows, :]

    put(left.at[chip], own_ref)
    for shift, ref in enumerate(row_refs, 1):
        put(left.at[lax.rem(chip + chips - shift, chips)], ref)
    for op, ref in enumerate(column_refs):
        mt, mb = divmod(op, ratio)
        source = lax.rem(target + chips - mt, chips)
        put(right.at[lax.rem(sub + ratio - mb, ratio), source], ref)

    lane = lax.broadcasted_iota(jnp.int32, (pairs, LANES), 1)
    low_half = lane < points
    last_row = (pairs - 1) * COLS
    low_lanes = lax.broadcasted_iota(jnp.int32, (COLS, LANES), 1) < points

    def finish(at):
        for t in range(2 * chips):
            here = at(t)
            value = here[last_row : last_row + COLS, :]
            if t + 1 < 2 * chips:
                extra = pltpu.roll(at(t + 1)[pairs * COLS :, :], points, 1)
                value = jnp.where(low_lanes, value, value + extra)
            else:
                value = jnp.where(low_lanes, value, 0.0)
            here[last_row : last_row + COLS, :] = value

    finish(lambda t: left.at[t // 2, t % 2])
    for b in range(ratio):
        finish(lambda t, b=b: right.at[b, t // 2, t % 2])

    def join(low, high):
        return (
            jnp.where(low_half, low, pltpu.roll(high, points, 1)),
            jnp.where(low_half, pltpu.roll(low, points, 1), high),
        )

    for f in range(NFREQ):
        lhs, rhs = [[], []], [[], []]
        for t in range(2 * chips):
            real, imag = (left.at[t // 2, t % 2][pl.ds(part * NFREQ + f, pairs, stride=COLS), :] for part in range(2))
            lhs[0] += join(real, imag)
            lhs[1] += join(imag, -real)
            for part in range(2):
                pick = pl.ds(part * NFREQ + f, pairs, stride=COLS)
                rhs[part] += join(*(right.at[b, t // 2, t % 2][pick, :] for b in range(2)))
        lhs_high, lhs_low = split(jnp.concatenate(lhs[0] + lhs[1], axis=0))
        rhs_high, rhs_low = split(jnp.concatenate(rhs[0] + rhs[1], axis=0))
        dot = functools.partial(
            lax.dot_general, dimension_numbers=CONTRACT_FIRST, preferred_element_type=jnp.float32
        )
        tile = dot(lhs_high, rhs_high) + (dot(lhs_high, rhs_low) + dot(lhs_low, rhs_high))
        tile = tile * scale
        out_ref[0, f] = tile[:points]
        out_ref[1, f] = tile[points:]


def body(signals, freq_bins):
    points, samples = signals.shape
    n_pt, n_tm = lax.axis_size("pt"), lax.axis_size("tm")
    ratio, chips = n_pt // n_tm, n_tm // 2
    where = lambda group, sub, chip, core: ((group * ratio + sub) * chips + chip) * 2 + core
    places = [
        (group, sub, chip, core)
        for group in range(n_tm)
        for sub in range(ratio)
        for chip in range(chips)
        for core in range(2)
    ]

    def permute(value, target):
        pairs = [(where(*place), where(*target(*place))) for place in places]
        return lax.ppermute(value, ("pt", "tm"), pairs)

    mine = project(signals, freq_bins)
    other = permute(mine, lambda g, s, x, c: (g, s, x, 1 - c))
    pt, tm = lax.axis_index("pt"), lax.axis_index("tm")
    is_first = tm % 2 == 0
    chip_block = jnp.concatenate(
        [jnp.where(is_first, mine, other), jnp.where(is_first, other, mine)], axis=0
    )
    row_blocks = [
        permute(chip_block, lambda g, s, x, c: (g, s, (x + m) % chips, c)) for m in range(1, chips)
    ]
    column_blocks = [
        permute(
            chip_block,
            lambda g, s, x, c: (2 * ((x + mt) % chips) + c, (s + mb) % ratio, g // 2, g % 2),
        )
        for mt in range(chips)
        for mb in range(ratio)
    ]
    place = jnp.stack([tm // 2, pt // ratio // 2, pt % ratio]).astype(jnp.int32)
    rows = mine.shape[0]
    segments = samples // HALF * n_tm - 1
    count = 1 + len(row_blocks) + len(column_blocks)
    return pl.pallas_call(
        functools.partial(tiles_kernel, chips, ratio, 1.0 / (segments * 0.375 * SEGLEN)),
        out_shape=jax.ShapeDtypeStruct((2, NFREQ, points, ratio * points), jnp.float32),
        in_specs=[pl.BlockSpec(memory_space=pltpu.SMEM)] + [pl.BlockSpec(memory_space=pltpu.VMEM)] * count,
        out_specs=pl.BlockSpec(memory_space=pltpu.VMEM),
        scratch_shapes=[
            pltpu.VMEM((chips, 2, rows, LANES), jnp.float32),
            pltpu.VMEM((ratio, chips, 2, rows, LANES), jnp.float32),
        ],
        name="tiles",
    )(place, chip_block, *row_blocks, *column_blocks)


def solution(mesh):
    in_specs = (P("pt", "tm"), P())
    out_specs = P(None, None, "pt", "tm")
    return jax.shard_map(body, mesh=mesh, in_specs=in_specs, out_specs=out_specs, check_vma=False)
```

```python
import functools
import math

import jax
import jax.numpy as jnp
from jax import lax
from jax.experimental import pallas as pl
from jax.experimental.pallas import tpu as pltpu
from jax.sharding import PartitionSpec as P

SEGLEN = 1024
HALF = SEGLEN // 2
NFREQ = 4
COLS = 2 * NFREQ
LANES = 128
VMEM_LIMIT = 16 << 20
SERIES = [(-1) ** n / math.factorial(2 * n) for n in range(8)]
CONTRACT_LAST = (((1,), (1,)), ((), ()))
CONTRACT_FIRST = (((0,), (0,)), ((), ()))


def cosine_of(steps):
    wrapped = ((steps + HALF) & (SEGLEN - 1)) - HALF
    size = jnp.abs(wrapped)
    folded = size > HALF // 2
    size = jnp.where(folded, HALF - size, size)
    angle = size.astype(jnp.float32) * (2.0 * math.pi / SEGLEN)
    square = angle * angle
    value = jnp.full_like(square, SERIES[-1])
    for term in SERIES[-2::-1]:
        value = value * square + term
    return jnp.where(folded, -value, value)


def split(value):
    high = value.astype(jnp.bfloat16)
    low = (value - high.astype(jnp.float32)).astype(jnp.bfloat16)
    return high, low


def project_kernel(bins_hbm, signals_ref, out_ref, held, sems, bins_ref, bins_sem):
    pairs, width, _ = held.shape
    points = width // 2
    bins_copy = pltpu.make_async_copy(bins_hbm, bins_ref, bins_sem)
    bins_copy.start()
    copies = []
    for j in range(pairs):
        for h in range(2):
            copies.append(
                pltpu.make_async_copy(
                    signals_ref.at[:, pl.ds((j + pairs * h) * HALF, HALF)],
                    held.at[j, pl.ds(h * points, points), :],
                    sems.at[j, h],
                )
            )
            copies[-1].start()
    row = lax.broadcasted_iota(jnp.int32, (COLS, SEGLEN), 0)
    sample = lax.broadcasted_iota(jnp.int32, (COLS, SEGLEN), 1)
    window = 0.5 - 0.5 * cosine_of(sample)
    bins_copy.wait()
    bins = jnp.zeros((COLS, SEGLEN), jnp.int32)
    for f in range(NFREQ):
        bins = jnp.where(row % NFREQ == f, bins_ref[f], bins)
    quarter = jnp.where(row >= NFREQ, SEGLEN // 4, 0)
    table = window * cosine_of(sample * bins + quarter)
    high, low = split(jnp.concatenate([table[:, :HALF], table[:, HALF:]], axis=0))
    both = jnp.concatenate([high, low], axis=0)
    first, second = [], []
    step = 4 if pairs % 4 == 0 else 1
    for j in range(0, pairs, step):
        for copy in copies[2 * j : 2 * (j + step)]:
            copy.wait()
        block = jnp.concatenate([held[j + q] for q in range(step)], axis=0)
        block_high, block_low = split(block)
        main = lax.dot_general(both, block_high, CONTRACT_LAST, preferred_element_type=jnp.float32)
        rest = lax.dot_general(high, block_low, CONTRACT_LAST, preferred_element_type=jnp.float32)
        sums = main[: 2 * COLS] + main[2 * COLS :] + rest
        for q in range(step):
            first.append(sums[:COLS, q * width : (q + 1) * width])
            second.append(sums[COLS:, q * width : (q + 1) * width])
    for j in range(pairs - 1):
        out_ref[j * COLS : (j + 1) * COLS, :] = first[j] + second[j + 1]
    lane = lax.broadcasted_iota(jnp.int32, (COLS, width), 1)
    wrap = jnp.where(lane < points, pltpu.roll(second[0], points, 1), 0.0)
    out_ref[(pairs - 1) * COLS : pairs * COLS, :] = first[pairs - 1] + wrap
    out_ref[pairs * COLS :, :] = second[0]


def project(signals, freq_bins):
    points, samples = signals.shape
    pairs = samples // HALF // 2
    return pl.pallas_call(
        project_kernel,
        out_shape=jax.ShapeDtypeStruct(((pairs + 1) * COLS, 2 * points), jnp.float32),
        in_specs=[pl.BlockSpec(memory_space=pltpu.HBM)] * 2,
        out_specs=pl.BlockSpec(memory_space=pltpu.VMEM),
        scratch_shapes=[
            pltpu.VMEM((pairs, 2 * points, HALF), jnp.float32),
            pltpu.SemaphoreType.DMA((pairs, 2)),
            pltpu.SMEM((NFREQ,), jnp.int32),
            pltpu.SemaphoreType.DMA,
        ],
        compiler_params=pltpu.CompilerParams(vmem_limit_bytes=VMEM_LIMIT),
        name="project",
    )(freq_bins, signals)


def tiles_kernel(chips, ratio, scale, *refs):
    own_ref = refs[0]
    row_refs = refs[1:chips]
    column_refs = refs[chips : chips + chips * ratio]
    out_ref, left, right = refs[chips + chips * ratio :]
    pt, tm = lax.axis_index("pt"), lax.axis_index("tm")
    chip, target, sub = lax.div(tm, 2), lax.div(lax.div(pt, ratio), 2), lax.rem(pt, ratio)
    rows = left.shape[2]
    pairs = rows // COLS - 1
    points = LANES // 2

    def put(dst, src, sender):
        for c in range(2):
            dst[lax.rem(sender + c, 2)] = src[c * rows : (c + 1) * rows, :]

    core, column_core = lax.rem(tm, 2), lax.rem(lax.div(pt, ratio), 2)
    put(left.at[chip], own_ref, core)
    for shift, ref in enumerate(row_refs, 1):
        put(left.at[lax.rem(chip + chips - shift, chips)], ref, core)
    for op, ref in enumerate(column_refs):
        mt, mb = divmod(op, ratio)
        source = lax.rem(target + chips - mt, chips)
        put(right.at[lax.rem(sub + ratio - mb, ratio), source], ref, column_core)

    lane = lax.broadcasted_iota(jnp.int32, (pairs, LANES), 1)
    low_half = lane < points
    last_row = (pairs - 1) * COLS
    low_lanes = lax.broadcasted_iota(jnp.int32, (COLS, LANES), 1) < points

    def finish(at):
        for t in range(2 * chips):
            here = at(t)
            value = here[last_row : last_row + COLS, :]
            if t + 1 < 2 * chips:
                extra = pltpu.roll(at(t + 1)[pairs * COLS :, :], points, 1)
                value = jnp.where(low_lanes, value, value + extra)
            else:
                value = jnp.where(low_lanes, value, 0.0)
            here[last_row : last_row + COLS, :] = value

    finish(lambda t: left.at[t // 2, t % 2])
    for b in range(ratio):
        finish(lambda t, b=b: right.at[b, t // 2, t % 2])

    def join(low, high):
        return (
            jnp.where(low_half, low, pltpu.roll(high, points, 1)),
            jnp.where(low_half, pltpu.roll(low, points, 1), high),
        )

    for f in range(NFREQ):
        lhs, rhs = [[], []], [[], []]
        for t in range(2 * chips):
            real, imag = (left.at[t // 2, t % 2][pl.ds(part * NFREQ + f, pairs, stride=COLS), :] for part in range(2))
            lhs[0] += join(real, imag)
            lhs[1] += join(imag, -real)
            for part in range(2):
                pick = pl.ds(part * NFREQ + f, pairs, stride=COLS)
                rhs[part] += join(*(right.at[b, t // 2, t % 2][pick, :] for b in range(2)))
        lhs_high, lhs_low = split(jnp.concatenate(lhs[0] + lhs[1], axis=0))
        rhs_high, rhs_low = split(jnp.concatenate(rhs[0] + rhs[1], axis=0))
        dot = functools.partial(
            lax.dot_general, dimension_numbers=CONTRACT_FIRST, preferred_element_type=jnp.float32
        )
        tile = dot(lhs_high, rhs_high) + (dot(lhs_high, rhs_low) + dot(lhs_low, rhs_high))
        tile = tile * scale
        out_ref[0, f] = tile[:points]
        out_ref[1, f] = tile[points:]


def body(signals, freq_bins):
    points, samples = signals.shape
    n_pt, n_tm = lax.axis_size("pt"), lax.axis_size("tm")
    ratio, chips = n_pt // n_tm, n_tm // 2
    where = lambda group, sub, chip, core: ((group * ratio + sub) * chips + chip) * 2 + core
    places = [
        (group, sub, chip, core)
        for group in range(n_tm)
        for sub in range(ratio)
        for chip in range(chips)
        for core in range(2)
    ]

    def permute(value, target):
        pairs = [(where(*place), where(*target(*place))) for place in places]
        return lax.ppermute(value, ("pt", "tm"), pairs)

    mine = project(signals, freq_bins)
    other = permute(mine, lambda g, s, x, c: (g, s, x, 1 - c))
    chip_block = jnp.concatenate([mine, other], axis=0)
    row_blocks = [
        permute(chip_block, lambda g, s, x, c: (g, s, (x + m) % chips, c)) for m in range(1, chips)
    ]
    column_blocks = [
        permute(
            chip_block,
            lambda g, s, x, c: (2 * ((x + mt) % chips) + c, (s + mb) % ratio, g // 2, g % 2),
        )
        for mt in range(chips)
        for mb in range(ratio)
    ]
    rows = mine.shape[0]
    segments = samples // HALF * n_tm - 1
    count = 1 + len(row_blocks) + len(column_blocks)
    return pl.pallas_call(
        functools.partial(tiles_kernel, chips, ratio, 1.0 / (segments * 0.375 * SEGLEN)),
        out_shape=jax.ShapeDtypeStruct((2, NFREQ, points, ratio * points), jnp.float32),
        in_specs=[pl.BlockSpec(memory_space=pltpu.VMEM)] * count,
        out_specs=pl.BlockSpec(memory_space=pltpu.VMEM),
        scratch_shapes=[
            pltpu.VMEM((chips, 2, rows, LANES), jnp.float32),
            pltpu.VMEM((ratio, chips, 2, rows, LANES), jnp.float32),
        ],
        compiler_params=pltpu.CompilerParams(vmem_limit_bytes=VMEM_LIMIT),
        name="tiles",
    )(chip_block, *row_blocks, *column_blocks)


def solution(mesh):
    in_specs = (P("pt", "tm"), P())
    out_specs = P(None, None, "pt", "tm")
    return jax.shard_map(body, mesh=mesh, in_specs=in_specs, out_specs=out_specs, check_vma=False)
```

```python
import functools
import math

import jax
import jax.numpy as jnp
from jax import lax
from jax.experimental import pallas as pl
from jax.experimental.pallas import tpu as pltpu
from jax.sharding import PartitionSpec as P

SEGLEN = 1024
HALF = SEGLEN // 2
NFREQ = 4
COLS = 2 * NFREQ
LANES = 128
VMEM_LIMIT = 16 << 20
COLUMN_ROUNDS = (
    ((3, 1, 2, 0), (2, 3, 0, 1), (3, 1, 0, 2), (2, 3, 1, 0)),
    ((2, 0, 1, 3), (1, 0, 2, 3), (2, 0, 1, 3), (0, 1, 3, 2)),
)
SERIES = [(-1) ** n / math.factorial(2 * n) for n in range(8)]
CONTRACT_LAST = (((1,), (1,)), ((), ()))
CONTRACT_FIRST = (((0,), (0,)), ((), ()))


def cosine_of(steps):
    wrapped = ((steps + HALF) & (SEGLEN - 1)) - HALF
    size = jnp.abs(wrapped)
    folded = size > HALF // 2
    size = jnp.where(folded, HALF - size, size)
    angle = size.astype(jnp.float32) * (2.0 * math.pi / SEGLEN)
    square = angle * angle
    value = jnp.full_like(square, SERIES[-1])
    for term in SERIES[-2::-1]:
        value = value * square + term
    return jnp.where(folded, -value, value)


def split(value):
    high = value.astype(jnp.bfloat16)
    low = (value - high.astype(jnp.float32)).astype(jnp.bfloat16)
    return high, low


def project_kernel(bins_hbm, signals_ref, out_ref, held, sems, bins_ref, bins_sem):
    pairs, width, _ = held.shape
    points = width // 2
    bins_copy = pltpu.make_async_copy(bins_hbm, bins_ref, bins_sem)
    bins_copy.start()
    copies = []
    for j in range(pairs):
        for h in range(2):
            copies.append(
                pltpu.make_async_copy(
                    signals_ref.at[:, pl.ds((j + pairs * h) * HALF, HALF)],
                    held.at[j, pl.ds(h * points, points), :],
                    sems.at[j, h],
                )
            )
            copies[-1].start()
    row = lax.broadcasted_iota(jnp.int32, (COLS, SEGLEN), 0)
    sample = lax.broadcasted_iota(jnp.int32, (COLS, SEGLEN), 1)
    window = 0.5 - 0.5 * cosine_of(sample)
    bins_copy.wait()
    bins = jnp.zeros((COLS, SEGLEN), jnp.int32)
    for f in range(NFREQ):
        bins = jnp.where(row % NFREQ == f, bins_ref[f], bins)
    quarter = jnp.where(row >= NFREQ, SEGLEN // 4, 0)
    table = window * cosine_of(sample * bins + quarter)
    high, low = split(jnp.concatenate([table[:, :HALF], table[:, HALF:]], axis=0))
    both = jnp.concatenate([high, low], axis=0)
    first, second = [], []
    step = 4 if pairs % 4 == 0 else 1
    for j in range(0, pairs, step):
        for copy in copies[2 * j : 2 * (j + step)]:
            copy.wait()
        block = jnp.concatenate([held[j + q] for q in range(step)], axis=0)
        block_high, block_low = split(block)
        main = lax.dot_general(both, block_high, CONTRACT_LAST, preferred_element_type=jnp.float32)
        rest = lax.dot_general(high, block_low, CONTRACT_LAST, preferred_element_type=jnp.float32)
        sums = main[: 2 * COLS] + main[2 * COLS :] + rest
        for q in range(step):
            first.append(sums[:COLS, q * width : (q + 1) * width])
            second.append(sums[COLS:, q * width : (q + 1) * width])
    for j in range(pairs - 1):
        out_ref[j * COLS : (j + 1) * COLS, :] = first[j] + second[j + 1]
    lane = lax.broadcasted_iota(jnp.int32, (COLS, width), 1)
    wrap = jnp.where(lane < points, pltpu.roll(second[0], points, 1), 0.0)
    out_ref[(pairs - 1) * COLS : pairs * COLS, :] = first[pairs - 1] + wrap
    out_ref[pairs * COLS :, :] = second[0]


def in_hbm(value):
    return pltpu.with_memory_space_constraint(value, pltpu.HBM)


def project(signals, freq_bins):
    points, samples = signals.shape
    pairs = samples // HALF // 2
    return pl.pallas_call(
        project_kernel,
        out_shape=jax.ShapeDtypeStruct(((pairs + 1) * COLS, 2 * points), jnp.float32),
        in_specs=[pl.BlockSpec(memory_space=pltpu.HBM)] * 2,
        out_specs=pl.BlockSpec(memory_space=pltpu.VMEM),
        scratch_shapes=[
            pltpu.VMEM((pairs, 2 * points, HALF), jnp.float32),
            pltpu.SemaphoreType.DMA((pairs, 2)),
            pltpu.SMEM((NFREQ,), jnp.int32),
            pltpu.SemaphoreType.DMA,
        ],
        compiler_params=pltpu.CompilerParams(vmem_limit_bytes=VMEM_LIMIT),
        name="project",
    )(in_hbm(freq_bins), in_hbm(signals))


def lookup(values, device):
    total = 0
    for bit in range(max(values).bit_length()):
        word = 0
        for start in range(0, len(values), 32):
            packed = sum((v >> bit & 1) << n for n, v in enumerate(values[start : start + 32]))
            packed -= (packed >> 31) << 32
            here = jnp.int32(packed)
            word = here if start == 0 else jnp.where(device >= start, here, word)
        total += (lax.shift_right_logical(word, lax.rem(device, 32)) & 1) << bit
    return total


def tiles_kernel(rounds, chips, ratio, scale, *refs):
    own_ref = refs[0]
    count = sum(1 if is_row else ratio for is_row, _ in rounds)
    round_refs = list(refs[1 : 1 + count])
    out_ref, left, right = refs[1 + count :]
    tm = lax.axis_index("tm")
    pt = lax.axis_index("pt")
    device = pt * lax.axis_size("tm") + tm
    sub = lax.rem(pt, ratio)
    rows = left.shape[2]
    pairs = rows // COLS - 1
    points = LANES // 2

    def put(dst, src, sender):
        for c in range(2):
            dst[lax.rem(sender + c, 2)] = src[c * rows : (c + 1) * rows, :]

    put(left.at[lax.div(tm, 2)], own_ref, lax.rem(tm, 2))
    for is_row, targets in rounds:
        sources = [targets.index(d) for d in range(len(targets))]
        core = lookup([d % 2 for d in sources], device)
        chip = lookup([d // 2 % chips for d in sources], device)
        if is_row:
            put(left.at[chip], round_refs.pop(0), core)
        else:
            for m in range(ratio):
                put(right.at[lax.rem(sub + ratio - m, ratio), chip], round_refs.pop(0), core)

    lane = lax.broadcasted_iota(jnp.int32, (pairs, LANES), 1)
    low_half = lane < points
    last_row = (pairs - 1) * COLS
    low_lanes = lax.broadcasted_iota(jnp.int32, (COLS, LANES), 1) < points

    def finish(at):
        for t in range(2 * chips):
            here = at(t)
            value = here[last_row : last_row + COLS, :]
            if t + 1 < 2 * chips:
                extra = pltpu.roll(at(t + 1)[pairs * COLS :, :], points, 1)
                value = jnp.where(low_lanes, value, value + extra)
            else:
                value = jnp.where(low_lanes, value, 0.0)
            here[last_row : last_row + COLS, :] = value

    finish(lambda t: left.at[t // 2, t % 2])
    for b in range(ratio):
        finish(lambda t, b=b: right.at[b, t // 2, t % 2])

    def join(low, high):
        return (
            jnp.where(low_half, low, pltpu.roll(high, points, 1)),
            jnp.where(low_half, pltpu.roll(low, points, 1), high),
        )

    for f in range(NFREQ):
        lhs, rhs = [[], []], [[], []]
        for t in range(2 * chips):
            real, imag = (left.at[t // 2, t % 2][pl.ds(part * NFREQ + f, pairs, stride=COLS), :] for part in range(2))
            lhs[0] += join(real, imag)
            lhs[1] += join(imag, -real)
            for part in range(2):
                pick = pl.ds(part * NFREQ + f, pairs, stride=COLS)
                rhs[part] += join(*(right.at[b, t // 2, t % 2][pick, :] for b in range(2)))
        lhs_high, lhs_low = split(jnp.concatenate(lhs[0] + lhs[1], axis=0))
        rhs_high, rhs_low = split(jnp.concatenate(rhs[0] + rhs[1], axis=0))
        dot = functools.partial(
            lax.dot_general, dimension_numbers=CONTRACT_FIRST, preferred_element_type=jnp.float32
        )
        tile = dot(lhs_high, rhs_high) + (dot(lhs_high, rhs_low) + dot(lhs_low, rhs_high))
        tile = tile * scale
        out_ref[0, f] = tile[:points]
        out_ref[1, f] = tile[points:]


def plan_rounds(chips, ratio):
    cores = 2 * chips
    devices = [
        (group, sub, chip, core)
        for group in range(cores)
        for sub in range(ratio)
        for chip in range(chips)
        for core in range(2)
    ]
    number = {place: n for n, place in enumerate(devices)}
    rounds = []
    for m in range(chips):
        if chips == len(COLUMN_ROUNDS):
            groups = COLUMN_ROUNDS[m]
        else:
            order = [2 * ((x + m) % chips) + c for x in range(chips) for c in range(2)]
            groups = [order] * cores
        rounds.append((False, [
            number[groups[g][2 * x + c], s, g // 2, g % 2] for g, s, x, c in devices
        ]))
    for m in range(1, chips):
        rounds.append((True, [number[g, s, (x + m) % chips, c] for g, s, x, c in devices]))
    return rounds


def body(signals, freq_bins):
    points, samples = signals.shape
    n_pt, n_tm = lax.axis_size("pt"), lax.axis_size("tm")
    ratio, chips = n_pt // n_tm, n_tm // 2

    def permute(value, targets):
        return lax.ppermute(value, ("pt", "tm"), list(enumerate(targets)))

    def to_sub(value, m):
        pairs = [(n, n // ratio * ratio + (n + m) % ratio) for n in range(n_pt)]
        return lax.ppermute(value, "pt", pairs)

    mine = project(signals, freq_bins)
    other = permute(mine, [n ^ 1 for n in range(n_pt * n_tm)])
    chip_block = jnp.concatenate([mine, other], axis=0)
    rounds = plan_rounds(chips, ratio)
    blocks = []
    for is_row, targets in rounds:
        blocks.append(permute(chip_block, targets))
        if not is_row:
            column = blocks[-1]
            blocks += [to_sub(column, m) for m in range(1, ratio)]
    rows = mine.shape[0]
    segments = samples // HALF * n_tm - 1
    scale = 1.0 / (segments * 0.375 * SEGLEN)
    return pl.pallas_call(
        functools.partial(tiles_kernel, rounds, chips, ratio, scale),
        out_shape=jax.ShapeDtypeStruct((2, NFREQ, points, ratio * points), jnp.float32),
        in_specs=[pl.BlockSpec(memory_space=pltpu.VMEM)] * (1 + len(blocks)),
        out_specs=pl.BlockSpec(memory_space=pltpu.VMEM),
        scratch_shapes=[
            pltpu.VMEM((chips, 2, rows, LANES), jnp.float32),
            pltpu.VMEM((ratio, chips, 2, rows, LANES), jnp.float32),
        ],
        compiler_params=pltpu.CompilerParams(vmem_limit_bytes=VMEM_LIMIT),
        name="tiles",
    )(chip_block, *blocks)


def solution(mesh):
    in_specs = (P("pt", "tm"), P())
    out_specs = P(None, None, "pt", "tm")
    return jax.shard_map(body, mesh=mesh, in_specs=in_specs, out_specs=out_specs, check_vma=False)
```

```python
import functools
import math

import jax
import jax.numpy as jnp
from jax import lax
from jax.experimental import pallas as pl
from jax.experimental.pallas import tpu as pltpu
from jax.sharding import PartitionSpec as P

SEGLEN = 1024
HALF = SEGLEN // 2
NFREQ = 4
COLS = 2 * NFREQ
LANES = 128
VMEM_LIMIT = 16 << 20
SERIES = [(-1) ** n / math.factorial(2 * n) for n in range(8)]
CONTRACT_LAST = (((1,), (1,)), ((), ()))
CONTRACT_FIRST = (((0,), (0,)), ((), ()))


TUNED_ROUNDS = (
    (0, (
        ((3, 1, 0, 2), (3, 1, 0, 2)),
        ((2, 3, 1, 0), (2, 3, 1, 0)),
        ((3, 1, 0, 2), (1, 3, 0, 2)),
        ((0, 3, 2, 1), (2, 3, 1, 0)),
    )),
    (1, (
        ((2, 0, 1, 3), (0, 2, 1, 3)),
        ((0, 1, 2, 3), (1, 0, 3, 2)),
        ((0, 2, 3, 1), (2, 0, 3, 1)),
        ((2, 1, 0, 3), (1, 0, 2, 3)),
    )),
    (1, 0),
    (0, (
        ((2, 0, 1, 3), (2, 0, 1, 3)),
        ((1, 0, 2, 3), (1, 0, 2, 3)),
        ((0, 2, 1, 3), (2, 0, 1, 3)),
        ((1, 2, 3, 0), (0, 1, 3, 2)),
    )),
    (None, 1),
)


def cosine_of(steps):
    wrapped = ((steps + HALF) & (SEGLEN - 1)) - HALF
    size = jnp.abs(wrapped)
    folded = size > HALF // 2
    size = jnp.where(folded, HALF - size, size)
    angle = size.astype(jnp.float32) * (2.0 * math.pi / SEGLEN)
    square = angle * angle
    value = jnp.full_like(square, SERIES[-1])
    for term in SERIES[-2::-1]:
        value = value * square + term
    return jnp.where(folded, -value, value)


def split(value):
    high = value.astype(jnp.bfloat16)
    low = (value - high.astype(jnp.float32)).astype(jnp.bfloat16)
    return high, low


def project_kernel(bins_hbm, signals_ref, out_ref, held, sems, bins_ref, bins_sem):
    pairs, width, _ = held.shape
    points = width // 2
    bins_copy = pltpu.make_async_copy(bins_hbm, bins_ref, bins_sem)
    bins_copy.start()
    copies = []
    for j in range(pairs):
        for h in range(2):
            copies.append(
                pltpu.make_async_copy(
                    signals_ref.at[:, pl.ds((j + pairs * h) * HALF, HALF)],
                    held.at[j, pl.ds(h * points, points), :],
                    sems.at[j, h],
                )
            )
            copies[-1].start()
    row = lax.broadcasted_iota(jnp.int32, (COLS, SEGLEN), 0)
    sample = lax.broadcasted_iota(jnp.int32, (COLS, SEGLEN), 1)
    window = 0.5 - 0.5 * cosine_of(sample)
    bins_copy.wait()
    bins = jnp.zeros((COLS, SEGLEN), jnp.int32)
    for f in range(NFREQ):
        bins = jnp.where(row % NFREQ == f, bins_ref[f], bins)
    quarter = jnp.where(row >= NFREQ, SEGLEN // 4, 0)
    table = window * cosine_of(sample * bins + quarter)
    high, low = split(jnp.concatenate([table[:, :HALF], table[:, HALF:]], axis=0))
    both = jnp.concatenate([high, low], axis=0)
    first, second = [], []
    step = 4 if pairs % 4 == 0 else 1
    for j in range(0, pairs, step):
        for copy in copies[2 * j : 2 * (j + step)]:
            copy.wait()
        block = jnp.concatenate([held[j + q] for q in range(step)], axis=0)
        block_high, block_low = split(block)
        main = lax.dot_general(both, block_high, CONTRACT_LAST, preferred_element_type=jnp.float32)
        rest = lax.dot_general(high, block_low, CONTRACT_LAST, preferred_element_type=jnp.float32)
        sums = main[: 2 * COLS] + main[2 * COLS :] + rest
        for q in range(step):
            first.append(sums[:COLS, q * width : (q + 1) * width])
            second.append(sums[COLS:, q * width : (q + 1) * width])
    for j in range(pairs - 1):
        out_ref[j * COLS : (j + 1) * COLS, :] = first[j] + second[j + 1]
    lane = lax.broadcasted_iota(jnp.int32, (COLS, width), 1)
    wrap = jnp.where(lane < points, pltpu.roll(second[0], points, 1), 0.0)
    out_ref[(pairs - 1) * COLS : pairs * COLS, :] = first[pairs - 1] + wrap
    out_ref[pairs * COLS :, :] = second[0]


def in_hbm(value):
    return pltpu.with_memory_space_constraint(value, pltpu.HBM)


def project(signals, freq_bins):
    points, samples = signals.shape
    pairs = samples // HALF // 2
    return pl.pallas_call(
        project_kernel,
        out_shape=jax.ShapeDtypeStruct(((pairs + 1) * COLS, 2 * points), jnp.float32),
        in_specs=[pl.BlockSpec(memory_space=pltpu.HBM)] * 2,
        out_specs=pl.BlockSpec(memory_space=pltpu.VMEM),
        scratch_shapes=[
            pltpu.VMEM((pairs, 2 * points, HALF), jnp.float32),
            pltpu.SemaphoreType.DMA((pairs, 2)),
            pltpu.SMEM((NFREQ,), jnp.int32),
            pltpu.SemaphoreType.DMA,
        ],
        compiler_params=pltpu.CompilerParams(vmem_limit_bytes=VMEM_LIMIT),
        name="project",
    )(in_hbm(freq_bins), in_hbm(signals))


def lookup(values, device):
    total = 0
    for bit in range(max(values).bit_length()):
        word = 0
        for start in range(0, len(values), 32):
            packed = sum((v >> bit & 1) << n for n, v in enumerate(values[start : start + 32]))
            packed -= (packed >> 31) << 32
            here = jnp.int32(packed)
            word = here if start == 0 else jnp.where(device >= start, here, word)
        total += (lax.shift_right_logical(word, lax.rem(device, 32)) & 1) << bit
    return total


def tiles_kernel(origins, chips, ratio, scale, *refs):
    blocks = refs[: len(origins)]
    out_ref, left, right = refs[len(origins) :]
    pt, tm = lax.axis_index("pt"), lax.axis_index("tm")
    device = pt * lax.axis_size("tm") + tm
    sub = lax.rem(pt, ratio)
    rows = left.shape[2]
    pairs = rows // COLS - 1
    points = LANES // 2

    for (places, sources), ref in zip(origins, blocks, strict=True):
        core = lookup([source % 2 for source in sources], device)
        chip = lookup([source // 2 % chips for source in sources], device)
        if places is None:
            dst = left.at[chip]
        else:
            dst = right.at[lax.rem(sub + ratio - places, ratio), chip]
        for c in range(2):
            dst[lax.rem(core + c, 2)] = ref[c * rows : (c + 1) * rows, :]

    lane = lax.broadcasted_iota(jnp.int32, (pairs, LANES), 1)
    low_half = lane < points
    last_row = (pairs - 1) * COLS
    low_lanes = lax.broadcasted_iota(jnp.int32, (COLS, LANES), 1) < points

    def finish(at):
        for t in range(2 * chips):
            here = at(t)
            value = here[last_row : last_row + COLS, :]
            if t + 1 < 2 * chips:
                extra = pltpu.roll(at(t + 1)[pairs * COLS :, :], points, 1)
                value = jnp.where(low_lanes, value, value + extra)
            else:
                value = jnp.where(low_lanes, value, 0.0)
            here[last_row : last_row + COLS, :] = value

    finish(lambda t: left.at[t // 2, t % 2])
    for b in range(ratio):
        finish(lambda t, b=b: right.at[b, t // 2, t % 2])

    def join(low, high):
        return (
            jnp.where(low_half, low, pltpu.roll(high, points, 1)),
            jnp.where(low_half, pltpu.roll(low, points, 1), high),
        )

    for f in range(NFREQ):
        lhs, rhs = [[], []], [[], []]
        for t in range(2 * chips):
            real, imag = (left.at[t // 2, t % 2][pl.ds(part * NFREQ + f, pairs, stride=COLS), :] for part in range(2))
            lhs[0] += join(real, imag)
            lhs[1] += join(imag, -real)
            for part in range(2):
                pick = pl.ds(part * NFREQ + f, pairs, stride=COLS)
                rhs[part] += join(*(right.at[b, t // 2, t % 2][pick, :] for b in range(2)))
        lhs_high, lhs_low = split(jnp.concatenate(lhs[0] + lhs[1], axis=0))
        rhs_high, rhs_low = split(jnp.concatenate(rhs[0] + rhs[1], axis=0))
        dot = functools.partial(
            lax.dot_general, dimension_numbers=CONTRACT_FIRST, preferred_element_type=jnp.float32
        )
        tile = dot(lhs_high, rhs_high) + (dot(lhs_high, rhs_low) + dot(lhs_low, rhs_high))
        tile = tile * scale
        out_ref[0, f] = tile[:points]
        out_ref[1, f] = tile[points:]


def plan_rounds(chips, ratio):
    cores = 2 * chips
    devices = [
        (group, sub, chip, core)
        for group in range(cores)
        for sub in range(ratio)
        for chip in range(chips)
        for core in range(2)
    ]
    number = {place: n for n, place in enumerate(devices)}

    def column(places, groups):
        targets = [
            number[groups[g][s][2 * x + c], (s + places) % ratio, g // 2, g % 2] for g, s, x, c in devices
        ]
        return places, targets, None

    def row(shift):
        return None, [number[g, s, (x + shift) % chips, c] for g, s, x, c in devices], None

    if (chips, ratio) == (2, 2):
        return [
            row(what) if places is None
            else (places, None, what) if isinstance(what, int)
            else column(places, what)
            for places, what in TUNED_ROUNDS
        ]
    rounds = []
    for m in range(chips):
        order = [2 * ((x + m) % chips) + c for x in range(chips) for c in range(2)]
        rounds.append(column(0, [[order] * ratio] * cores))
    rounds += [row(shift) for shift in range(1, chips)]
    for places in range(1, ratio):
        rounds += [(places, None, m) for m in range(chips)]
    return rounds


def body(signals, freq_bins):
    points, samples = signals.shape
    n_pt, n_tm = lax.axis_size("pt"), lax.axis_size("tm")
    ratio, chips = n_pt // n_tm, n_tm // 2
    devices = range(n_pt * n_tm)

    def permute(value, targets):
        return lax.ppermute(value, ("pt", "tm"), list(enumerate(targets)))

    def moved(n, places):
        sub = n // n_tm % ratio
        return n + ((sub + places) % ratio - sub) * n_tm

    mine = project(signals, freq_bins)
    other = permute(mine, [n ^ 1 for n in devices])
    chip_block = jnp.concatenate([mine, other], axis=0)
    blocks, origins = [], []
    for places, targets, passed in plan_rounds(chips, ratio):
        if passed is None:
            blocks.append(permute(chip_block, targets))
            origins.append((places, [targets.index(n) for n in devices]))
        else:
            blocks.append(permute(blocks[passed], [moved(n, places) for n in devices]))
            before = origins[passed][1]
            origins.append((places, [before[moved(n, -places)] for n in devices]))
    blocks.append(chip_block)
    origins.append((None, list(devices)))
    blocks, origins = blocks[::-1], origins[::-1]
    segments = samples // HALF * n_tm - 1
    scale = 1.0 / (segments * 0.375 * SEGLEN)
    rows = mine.shape[0]
    return pl.pallas_call(
        functools.partial(tiles_kernel, origins, chips, ratio, scale),
        out_shape=jax.ShapeDtypeStruct((2, NFREQ, points, ratio * points), jnp.float32),
        in_specs=[pl.BlockSpec(memory_space=pltpu.VMEM)] * len(blocks),
        out_specs=pl.BlockSpec(memory_space=pltpu.VMEM),
        scratch_shapes=[
            pltpu.VMEM((chips, 2, rows, LANES), jnp.float32),
            pltpu.VMEM((ratio, chips, 2, rows, LANES), jnp.float32),
        ],
        compiler_params=pltpu.CompilerParams(vmem_limit_bytes=VMEM_LIMIT),
        name="tiles",
    )(*blocks)


def solution(mesh):
    in_specs = (P("pt", "tm"), P())
    out_specs = P(None, None, "pt", "tm")
    return jax.shard_map(body, mesh=mesh, in_specs=in_specs, out_specs=out_specs, check_vma=False)
```

```python
import functools
import math

import jax
import jax.numpy as jnp
from jax import lax
from jax.experimental import pallas as pl
from jax.experimental.pallas import tpu as pltpu
from jax.sharding import PartitionSpec as P

SEGLEN = 1024
HALF = SEGLEN // 2
NFREQ = 4
COLS = 2 * NFREQ
LANES = 128
VMEM_LIMIT = 16 << 20
SERIES = [(-1) ** n / math.factorial(2 * n) for n in range(8)]
CONTRACT_LAST = (((1,), (1,)), ((), ()))
CONTRACT_FIRST = (((0,), (0,)), ((), ()))


TUNED_ROUNDS = (
    (0, (
        ((3, 1, 0, 2), (3, 1, 0, 2)),
        ((2, 3, 1, 0), (2, 3, 1, 0)),
        ((3, 1, 0, 2), (1, 3, 0, 2)),
        ((0, 3, 2, 1), (2, 3, 1, 0)),
    )),
    (1, (
        ((2, 0, 1, 3), (0, 2, 1, 3)),
        ((0, 1, 2, 3), (1, 0, 3, 2)),
        ((0, 2, 3, 1), (2, 0, 3, 1)),
        ((2, 1, 0, 3), (1, 0, 2, 3)),
    )),
    (1, 0),
    (0, (
        ((2, 0, 1, 3), (2, 0, 1, 3)),
        ((1, 0, 2, 3), (1, 0, 2, 3)),
        ((0, 2, 1, 3), (2, 0, 1, 3)),
        ((1, 2, 3, 0), (0, 1, 3, 2)),
    )),
    (None, 1),
)


def cosine_of(steps):
    wrapped = ((steps + HALF) & (SEGLEN - 1)) - HALF
    size = jnp.abs(wrapped)
    folded = size > HALF // 2
    size = jnp.where(folded, HALF - size, size)
    angle = size.astype(jnp.float32) * (2.0 * math.pi / SEGLEN)
    square = angle * angle
    value = jnp.full_like(square, SERIES[-1])
    for term in SERIES[-2::-1]:
        value = value * square + term
    return jnp.where(folded, -value, value)


def split(value):
    high = value.astype(jnp.bfloat16)
    low = (value - high.astype(jnp.float32)).astype(jnp.bfloat16)
    return high, low


def project_kernel(bins_hbm, signals_ref, out_ref, held, sems, bins_ref, bins_sem):
    pairs, width, _ = held.shape
    points = width // 2
    bins_copy = pltpu.make_async_copy(bins_hbm, bins_ref, bins_sem)
    bins_copy.start()
    copies = []
    for j in range(pairs):
        for h in range(2):
            copies.append(
                pltpu.make_async_copy(
                    signals_ref.at[:, pl.ds((j + pairs * h) * HALF, HALF)],
                    held.at[j, pl.ds(h * points, points), :],
                    sems.at[j, h],
                )
            )
            copies[-1].start()
    row = lax.broadcasted_iota(jnp.int32, (COLS, SEGLEN), 0)
    sample = lax.broadcasted_iota(jnp.int32, (COLS, SEGLEN), 1)
    window = 0.5 - 0.5 * cosine_of(sample)
    bins_copy.wait()
    bins = jnp.zeros((COLS, SEGLEN), jnp.int32)
    for f in range(NFREQ):
        bins = jnp.where(row % NFREQ == f, bins_ref[f], bins)
    quarter = jnp.where(row >= NFREQ, SEGLEN // 4, 0)
    table = window * cosine_of(sample * bins + quarter)
    high, low = split(jnp.concatenate([table[:, :HALF], table[:, HALF:]], axis=0))
    both = jnp.concatenate([high, low], axis=0)
    first, second = [], []
    step = 4 if pairs % 4 == 0 else 1
    for j in range(0, pairs, step):
        for copy in copies[2 * j : 2 * (j + step)]:
            copy.wait()
        block = jnp.concatenate([held[j + q] for q in range(step)], axis=0)
        block_high, block_low = split(block)
        main = lax.dot_general(both, block_high, CONTRACT_LAST, preferred_element_type=jnp.float32)
        rest = lax.dot_general(high, block_low, CONTRACT_LAST, preferred_element_type=jnp.float32)
        sums = main[: 2 * COLS] + main[2 * COLS :] + rest
        for q in range(step):
            first.append(sums[:COLS, q * width : (q + 1) * width])
            second.append(sums[COLS:, q * width : (q + 1) * width])
    for j in range(pairs - 1):
        out_ref[j * COLS : (j + 1) * COLS, :] = first[j] + second[j + 1]
    lane = lax.broadcasted_iota(jnp.int32, (COLS, width), 1)
    wrap = jnp.where(lane < points, pltpu.roll(second[0], points, 1), 0.0)
    out_ref[(pairs - 1) * COLS : pairs * COLS, :] = first[pairs - 1] + wrap
    out_ref[pairs * COLS :, :] = second[0]


def in_hbm(value):
    return pltpu.with_memory_space_constraint(value, pltpu.HBM)


def project(signals, freq_bins):
    points, samples = signals.shape
    pairs = samples // HALF // 2
    return pl.pallas_call(
        project_kernel,
        out_shape=jax.ShapeDtypeStruct(((pairs + 1) * COLS, 2 * points), jnp.float32),
        in_specs=[pl.BlockSpec(memory_space=pltpu.HBM)] * 2,
        out_specs=pl.BlockSpec(memory_space=pltpu.VMEM),
        scratch_shapes=[
            pltpu.VMEM((pairs, 2 * points, HALF), jnp.float32),
            pltpu.SemaphoreType.DMA((pairs, 2)),
            pltpu.SMEM((NFREQ,), jnp.int32),
            pltpu.SemaphoreType.DMA,
        ],
        compiler_params=pltpu.CompilerParams(vmem_limit_bytes=VMEM_LIMIT),
        name="project",
    )(in_hbm(freq_bins), in_hbm(signals))


def lookup(values, device):
    total = 0
    for bit in range(max(values).bit_length()):
        word = 0
        for start in range(0, len(values), 32):
            packed = sum((v >> bit & 1) << n for n, v in enumerate(values[start : start + 32]))
            packed -= (packed >> 31) << 32
            here = jnp.int32(packed)
            word = here if start == 0 else jnp.where(device >= start, here, word)
        total += (lax.shift_right_logical(word, lax.rem(device, 32)) & 1) << bit
    return total


def join(low, high):
    points = LANES // 2
    is_low = lax.broadcasted_iota(jnp.int32, low.shape, 1) < points
    return (
        jnp.where(is_low, low, pltpu.roll(high, points, 1)),
        jnp.where(is_low, pltpu.roll(low, points, 1), high),
    )


def place_of(sources, chips, device):
    chip = lookup([source // 2 % chips for source in sources], device)
    return chip, lookup([source % 2 for source in sources], device)


def put(dst, src, sender):
    rows = src.shape[0] // 2
    for c in range(2):
        dst[lax.rem(sender + c, 2)] = src[c * rows : (c + 1) * rows, :]


def this_device():
    pt, tm = lax.axis_index("pt"), lax.axis_index("tm")
    return pt * lax.axis_size("tm") + tm, pt, tm


def prepare_kernel(rows_from, columns_from, chips, ratio, *refs):
    own_ref = refs[0]
    column_refs = refs[1 : len(columns_from)]
    row_refs = refs[len(columns_from) : len(rows_from) + len(columns_from)]
    lhs_high_ref, lhs_low_ref, rhs_ref, tail_ref, left, right = refs[len(rows_from) + len(columns_from) :]
    device, pt, tm = this_device()
    sub = lax.rem(pt, ratio)
    times = 2 * chips
    pairs = left.shape[2] // COLS - 1
    points = LANES // 2

    put(left.at[lax.div(tm, 2)], own_ref, lax.rem(tm, 2))
    for sources, ref in zip(rows_from, row_refs, strict=True):
        chip, core = place_of(sources, chips, device)
        put(left.at[chip], ref, core)
    for (m, sources), ref in zip(columns_from[:-1], column_refs, strict=True):
        chip, core = place_of(sources, chips, device)
        put(right.at[lax.rem(sub + ratio - m, ratio), chip], ref, core)
    m, sources = columns_from[-1]
    last_sub = lax.rem(sub + ratio - m, ratio)
    last_chip, _ = place_of(sources, chips, device)

    ends = pl.ds((pairs - 1) * COLS, COLS)
    heads = pl.ds(pairs * COLS, COLS)
    is_low = lax.broadcasted_iota(jnp.int32, (COLS, LANES), 1) < points

    def finish(at, missing):
        for t in range(times):
            value = at(t)[ends, :]
            if t + 1 < times:
                extra = pltpu.roll(at(t + 1)[heads, :], points, 1)
                if t % 2:
                    extra = jnp.where(missing(t // 2 + 1), 0.0, extra)
                at(t)[ends, :] = jnp.where(is_low, value, value + extra)
            else:
                at(t)[ends, :] = jnp.where(is_low, value, 0.0)

    after = right.at[last_sub, jnp.minimum(last_chip + 1, chips - 1), 0]
    tail_ref[...] = pltpu.roll(after[heads, :], points, 1)
    finish(lambda t: left.at[t // 2, t % 2], lambda chip: False)
    for b in range(ratio):
        finish(
            lambda t, b=b: right.at[b, t // 2, t % 2],
            lambda chip, b=b: jnp.logical_and(last_sub == b, last_chip == chip),
        )

    for f in range(NFREQ):
        lhs, rhs = [[], []], [[], []]
        for t in range(times):
            real, imag = (
                left.at[t // 2, t % 2][pl.ds(part * NFREQ + f, pairs, stride=COLS), :]
                for part in range(2)
            )
            lhs[0] += join(real, imag)
            lhs[1] += join(imag, -real)
            for part in range(2):
                pick = pl.ds(part * NFREQ + f, pairs, stride=COLS)
                rhs[part] += join(*(right.at[b, t // 2, t % 2][pick, :] for b in range(ratio)))
        lhs_high_ref[f], lhs_low_ref[f] = split(jnp.concatenate(lhs[0] + lhs[1], axis=0).T)
        rhs_ref[f] = jnp.concatenate(rhs[0] + rhs[1], axis=0)


def tiles_kernel(
    last_from, chips, ratio, scale, lhs_high_ref, lhs_low_ref, rhs_ref, tail_ref, last_ref, out_ref, last
):
    device, pt, _ = this_device()
    times = 2 * chips
    pairs = last.shape[1] // COLS - 1
    points = LANES // 2
    m, sources = last_from
    is_first = lax.rem(lax.rem(pt, ratio) + ratio - m, ratio) == 0
    last_chip, core = place_of(sources, chips, device)
    put(last, last_ref, core)

    ends = pl.ds((pairs - 1) * COLS, COLS)
    heads = pl.ds(pairs * COLS, COLS)
    is_low = lax.broadcasted_iota(jnp.int32, (COLS, LANES), 1) < points
    value = last[0, ends, :]
    last[0, ends, :] = jnp.where(is_low, value, value + pltpu.roll(last[1, heads, :], points, 1))
    value = last[1, ends, :]
    ended = jnp.where(last_chip == chips - 1, 0.0, value + tail_ref[...])
    last[1, ends, :] = jnp.where(is_low, value, ended)

    lane = lax.broadcasted_iota(jnp.int32, (pairs, LANES), 1)
    mine = jnp.where(is_first, lane, LANES - 1 - lane) < points
    from_here = [jnp.logical_and(mine, last_chip == chip) for chip in range(chips)]
    end_row = lax.broadcasted_iota(jnp.int32, (pairs, LANES), 0) == pairs - 1
    head = last[0, heads, :]
    head = jnp.where(is_first, head, pltpu.roll(head, points, 1))
    dot = functools.partial(jnp.dot, preferred_element_type=jnp.float32)
    for f in range(NFREQ):
        rhs = []
        for part in range(2):
            column = part * NFREQ + f
            new = []
            for c in range(2):
                picked = last[c, pl.ds(column, pairs, stride=COLS), :]
                turned = pltpu.roll(picked, points, 1)
                new.append((jnp.where(is_first, picked, turned), jnp.where(is_first, turned, picked)))
            for t in range(times):
                for h in range(2):
                    start = ((part * times + t) * 2 + h) * pairs
                    value = rhs_ref[f, start : start + pairs, :]
                    if h == 1 and t % 2 == 1 and t + 1 < times:
                        here = jnp.logical_and(end_row, from_here[t // 2 + 1])
                        value = value + jnp.where(here, head[column : column + 1, :], 0.0)
                    rhs.append(jnp.where(from_here[t // 2], new[t % 2][h], value))
        rhs_high, rhs_low = split(jnp.concatenate(rhs, axis=0))
        high, low = lhs_high_ref[f], lhs_low_ref[f]
        tile = dot(high, rhs_high) + (dot(high, rhs_low) + dot(low, rhs_high))
        tile = tile * scale
        out_ref[0, f] = tile[:points]
        out_ref[1, f] = tile[points:]


def plan_rounds(chips, ratio):
    cores = 2 * chips
    devices = [
        (group, sub, chip, core)
        for group in range(cores)
        for sub in range(ratio)
        for chip in range(chips)
        for core in range(2)
    ]
    number = {place: n for n, place in enumerate(devices)}

    def column(places, groups):
        targets = [
            number[groups[g][s][2 * x + c], (s + places) % ratio, g // 2, g % 2] for g, s, x, c in devices
        ]
        return places, targets, None

    def row(shift):
        return None, [number[g, s, (x + shift) % chips, c] for g, s, x, c in devices], None

    if (chips, ratio) == (2, 2):
        return [
            row(what) if places is None
            else (places, None, what) if isinstance(what, int)
            else column(places, what)
            for places, what in TUNED_ROUNDS
        ]
    rounds = []
    for m in range(chips):
        order = [2 * ((x + m) % chips) + c for x in range(chips) for c in range(2)]
        rounds.append(column(0, [[order] * ratio] * cores))
    rounds += [row(shift) for shift in range(1, chips)]
    for places in range(1, ratio):
        rounds += [(places, None, m) for m in range(chips)]
    return rounds


def body(signals, freq_bins):
    points, samples = signals.shape
    n_pt, n_tm = lax.axis_size("pt"), lax.axis_size("tm")
    ratio, chips = n_pt // n_tm, n_tm // 2
    devices = range(n_pt * n_tm)

    def permute(value, targets):
        return lax.ppermute(value, ("pt", "tm"), list(enumerate(targets)))

    def moved(n, places):
        sub = n // n_tm % ratio
        return n + ((sub + places) % ratio - sub) * n_tm

    mine = project(signals, freq_bins)
    other = permute(mine, [n ^ 1 for n in devices])
    chip_block = jnp.concatenate([mine, other], axis=0)
    blocks, origins = [], []
    plan = plan_rounds(chips, ratio)
    for places, targets, passed in plan:
        if passed is None:
            blocks.append(permute(chip_block, targets))
            origins.append((places, [targets.index(n) for n in devices]))
        else:
            blocks.append(permute(blocks[passed], [moved(n, places) for n in devices]))
            before = origins[passed][1]
            origins.append((places, [before[moved(n, -places)] for n in devices]))
    *_, last = (n for n, (places, targets, _) in enumerate(plan) if places is not None and targets is None)
    order = [n for n in range(len(plan)) if n != last] + [last]
    rows = [blocks[n] for n in order if origins[n][0] is None]
    rows_from = [origins[n][1] for n in order if origins[n][0] is None]
    columns = [blocks[n] for n in order if origins[n][0] is not None]
    columns_from = [origins[n] for n in order if origins[n][0] is not None]
    depth = mine.shape[0] - COLS
    depth = depth // COLS * 2 * 2 * n_tm
    segments = samples // HALF * n_tm - 1
    params = pltpu.CompilerParams(vmem_limit_bytes=VMEM_LIMIT)
    in_vmem = pl.BlockSpec(memory_space=pltpu.VMEM)
    block = (2, mine.shape[0], LANES)
    side = jax.ShapeDtypeStruct((NFREQ, LANES, depth), jnp.bfloat16)
    *sides, tail = pl.pallas_call(
        functools.partial(prepare_kernel, rows_from, columns_from, chips, ratio),
        out_shape=[
            side,
            side,
            jax.ShapeDtypeStruct((NFREQ, depth, LANES), jnp.float32),
            jax.ShapeDtypeStruct((COLS, LANES), jnp.float32),
        ],
        in_specs=[in_vmem] * (len(rows) + len(columns)),
        out_specs=[in_vmem] * 4,
        scratch_shapes=[
            pltpu.VMEM((chips, *block), jnp.float32),
            pltpu.VMEM((ratio, chips, *block), jnp.float32),
        ],
        compiler_params=params,
        name="prepare",
    )(chip_block, *columns[:-1], *rows)
    return pl.pallas_call(
        functools.partial(tiles_kernel, columns_from[-1], chips, ratio, 1.0 / (segments * 0.375 * SEGLEN)),
        out_shape=jax.ShapeDtypeStruct((2, NFREQ, points, ratio * points), jnp.float32),
        in_specs=[in_vmem] * 5,
        out_specs=in_vmem,
        scratch_shapes=[pltpu.VMEM(block, jnp.float32)],
        compiler_params=params,
        name="tiles",
    )(*sides, tail, columns[-1])


def solution(mesh):
    in_specs = (P("pt", "tm"), P())
    out_specs = P(None, None, "pt", "tm")
    return jax.shard_map(body, mesh=mesh, in_specs=in_specs, out_specs=out_specs, check_vma=False)
```

```python
import functools
import math

import jax
import jax.numpy as jnp
from jax import lax
from jax.experimental import pallas as pl
from jax.experimental.pallas import tpu as pltpu
from jax.sharding import PartitionSpec as P

SEGLEN = 1024
HALF = SEGLEN // 2
NFREQ = 4
COLS = 2 * NFREQ
LANES = 128
VMEM_LIMIT = 16 << 20
SERIES = [(-1) ** n / math.factorial(2 * n) for n in range(8)]
CONTRACT_LAST = (((1,), (1,)), ((), ()))
CONTRACT_FIRST = (((0,), (0,)), ((), ()))


TUNED_ROUNDS = (
    (0, (
        ((3, 1, 0, 2), (3, 1, 0, 2)),
        ((2, 3, 1, 0), (2, 3, 1, 0)),
        ((3, 0, 1, 2), (0, 3, 1, 2)),
        ((0, 3, 2, 1), (3, 2, 1, 0)),
    )),
    (1, 0),
    (1, (
        ((2, 0, 1, 3), (0, 2, 1, 3)),
        ((0, 1, 2, 3), (1, 0, 3, 2)),
        ((1, 2, 3, 0), (2, 1, 3, 0)),
        ((2, 1, 0, 3), (1, 0, 3, 2)),
    )),
    (0, (
        ((2, 0, 1, 3), (2, 0, 1, 3)),
        ((1, 0, 2, 3), (1, 0, 2, 3)),
        ((2, 1, 0, 3), (2, 1, 0, 3)),
        ((2, 1, 3, 0), (1, 0, 3, 2)),
    )),
    (None, 1),
)


def cosine_of(steps):
    wrapped = ((steps + HALF) & (SEGLEN - 1)) - HALF
    size = jnp.abs(wrapped)
    folded = size > HALF // 2
    size = jnp.where(folded, HALF - size, size)
    angle = size.astype(jnp.float32) * (2.0 * math.pi / SEGLEN)
    square = angle * angle
    value = jnp.full_like(square, SERIES[-1])
    for term in SERIES[-2::-1]:
        value = value * square + term
    return jnp.where(folded, -value, value)


def split(value):
    high = value.astype(jnp.bfloat16)
    low = (value - high.astype(jnp.float32)).astype(jnp.bfloat16)
    return high, low


def project_kernel(bins_hbm, signals_ref, out_ref, held, sems, bins_ref, bins_sem):
    pairs, width, _ = held.shape
    points = width // 2
    bins_copy = pltpu.make_async_copy(bins_hbm, bins_ref, bins_sem)
    bins_copy.start()
    copies = []
    for j in range(pairs):
        for h in range(2):
            copies.append(
                pltpu.make_async_copy(
                    signals_ref.at[:, pl.ds((j + pairs * h) * HALF, HALF)],
                    held.at[j, pl.ds(h * points, points), :],
                    sems.at[j, h],
                )
            )
            copies[-1].start()
    row = lax.broadcasted_iota(jnp.int32, (COLS, SEGLEN), 0)
    sample = lax.broadcasted_iota(jnp.int32, (COLS, SEGLEN), 1)
    window = 0.5 - 0.5 * cosine_of(sample)
    bins_copy.wait()
    bins = jnp.zeros((COLS, SEGLEN), jnp.int32)
    for f in range(NFREQ):
        bins = jnp.where(row % NFREQ == f, bins_ref[f], bins)
    quarter = jnp.where(row >= NFREQ, SEGLEN // 4, 0)
    table = window * cosine_of(sample * bins + quarter)
    high, low = split(jnp.concatenate([table[:, :HALF], table[:, HALF:]], axis=0))
    both = jnp.concatenate([high, low], axis=0)
    first, second = [], []
    step = 4 if pairs % 4 == 0 else 1
    for j in range(0, pairs, step):
        for copy in copies[2 * j : 2 * (j + step)]:
            copy.wait()
        block = jnp.concatenate([held[j + q] for q in range(step)], axis=0)
        block_high, block_low = split(block)
        main = lax.dot_general(both, block_high, CONTRACT_LAST, preferred_element_type=jnp.float32)
        rest = lax.dot_general(high, block_low, CONTRACT_LAST, preferred_element_type=jnp.float32)
        sums = main[: 2 * COLS] + main[2 * COLS :] + rest
        for q in range(step):
            first.append(sums[:COLS, q * width : (q + 1) * width])
            second.append(sums[COLS:, q * width : (q + 1) * width])
    for j in range(pairs - 1):
        out_ref[j * COLS : (j + 1) * COLS, :] = first[j] + second[j + 1]
    lane = lax.broadcasted_iota(jnp.int32, (COLS, width), 1)
    wrap = jnp.where(lane < points, pltpu.roll(second[0], points, 1), 0.0)
    out_ref[(pairs - 1) * COLS : pairs * COLS, :] = first[pairs - 1] + wrap
    out_ref[pairs * COLS :, :] = second[0]


def in_hbm(value):
    return pltpu.with_memory_space_constraint(value, pltpu.HBM)


def project(signals, freq_bins):
    points, samples = signals.shape
    pairs = samples // HALF // 2
    return pl.pallas_call(
        project_kernel,
        out_shape=jax.ShapeDtypeStruct(((pairs + 1) * COLS, 2 * points), jnp.float32),
        in_specs=[pl.BlockSpec(memory_space=pltpu.HBM)] * 2,
        out_specs=pl.BlockSpec(memory_space=pltpu.VMEM),
        scratch_shapes=[
            pltpu.VMEM((pairs, 2 * points, HALF), jnp.float32),
            pltpu.SemaphoreType.DMA((pairs, 2)),
            pltpu.SMEM((NFREQ,), jnp.int32),
            pltpu.SemaphoreType.DMA,
        ],
        compiler_params=pltpu.CompilerParams(vmem_limit_bytes=VMEM_LIMIT),
        name="project",
    )(in_hbm(freq_bins), in_hbm(signals))


def lookup(values, device):
    total = 0
    for bit in range(max(values).bit_length()):
        word = 0
        for start in range(0, len(values), 32):
            packed = sum((v >> bit & 1) << n for n, v in enumerate(values[start : start + 32]))
            packed -= (packed >> 31) << 32
            here = jnp.int32(packed)
            word = here if start == 0 else jnp.where(device >= start, here, word)
        total += (lax.shift_right_logical(word, lax.rem(device, 32)) & 1) << bit
    return total


def tiles_kernel(origins, chips, ratio, scale, *refs):
    blocks = refs[: len(origins)]
    out_ref, left, right = refs[len(origins) :]
    pt, tm = lax.axis_index("pt"), lax.axis_index("tm")
    device = pt * lax.axis_size("tm") + tm
    sub = lax.rem(pt, ratio)
    rows = left.shape[2]
    pairs = rows // COLS - 1
    points = LANES // 2

    for (places, sources), ref in zip(origins, blocks, strict=True):
        core = lookup([source % 2 for source in sources], device)
        chip = lookup([source // 2 % chips for source in sources], device)
        if places is None:
            dst = left.at[chip]
        else:
            dst = right.at[lax.rem(sub + ratio - places, ratio), chip]
        for c in range(2):
            dst[lax.rem(core + c, 2)] = ref[c * rows : (c + 1) * rows, :]

    lane = lax.broadcasted_iota(jnp.int32, (pairs, LANES), 1)
    low_half = lane < points
    last_row = (pairs - 1) * COLS
    low_lanes = lax.broadcasted_iota(jnp.int32, (COLS, LANES), 1) < points

    def finish(at):
        for t in range(2 * chips):
            here = at(t)
            value = here[last_row : last_row + COLS, :]
            if t + 1 < 2 * chips:
                extra = pltpu.roll(at(t + 1)[pairs * COLS :, :], points, 1)
                value = jnp.where(low_lanes, value, value + extra)
            else:
                value = jnp.where(low_lanes, value, 0.0)
            here[last_row : last_row + COLS, :] = value

    finish(lambda t: left.at[t // 2, t % 2])
    for b in range(ratio):
        finish(lambda t, b=b: right.at[b, t // 2, t % 2])

    def join(low, high):
        return (
            jnp.where(low_half, low, pltpu.roll(high, points, 1)),
            jnp.where(low_half, pltpu.roll(low, points, 1), high),
        )

    for f in range(NFREQ):
        lhs, rhs = [[], []], [[], []]
        for t in range(2 * chips):
            real, imag = (left.at[t // 2, t % 2][pl.ds(part * NFREQ + f, pairs, stride=COLS), :] for part in range(2))
            lhs[0] += join(real, imag)
            lhs[1] += join(imag, -real)
            for part in range(2):
                pick = pl.ds(part * NFREQ + f, pairs, stride=COLS)
                rhs[part] += join(*(right.at[b, t // 2, t % 2][pick, :] for b in range(2)))
        lhs_high, lhs_low = split(jnp.concatenate(lhs[0] + lhs[1], axis=0))
        rhs_high, rhs_low = split(jnp.concatenate(rhs[0] + rhs[1], axis=0))
        dot = functools.partial(
            lax.dot_general, dimension_numbers=CONTRACT_FIRST, preferred_element_type=jnp.float32
        )
        tile = dot(lhs_high, rhs_high) + (dot(lhs_high, rhs_low) + dot(lhs_low, rhs_high))
        tile = tile * scale
        out_ref[0, f] = tile[:points]
        out_ref[1, f] = tile[points:]


def plan_rounds(chips, ratio):
    cores = 2 * chips
    devices = [
        (group, sub, chip, core)
        for group in range(cores)
        for sub in range(ratio)
        for chip in range(chips)
        for core in range(2)
    ]
    number = {place: n for n, place in enumerate(devices)}

    def column(places, groups):
        targets = [
            number[groups[g][s][2 * x + c], (s + places) % ratio, g // 2, g % 2] for g, s, x, c in devices
        ]
        return places, targets, None

    def row(shift):
        return None, [number[g, s, (x + shift) % chips, c] for g, s, x, c in devices], None

    if (chips, ratio) == (2, 2):
        return [
            row(what) if places is None
            else (places, None, what) if isinstance(what, int)
            else column(places, what)
            for places, what in TUNED_ROUNDS
        ]
    rounds = []
    for m in range(chips):
        order = [2 * ((x + m) % chips) + c for x in range(chips) for c in range(2)]
        rounds.append(column(0, [[order] * ratio] * cores))
    rounds += [row(shift) for shift in range(1, chips)]
    for places in range(1, ratio):
        rounds += [(places, None, m) for m in range(chips)]
    return rounds


def body(signals, freq_bins):
    points, samples = signals.shape
    n_pt, n_tm = lax.axis_size("pt"), lax.axis_size("tm")
    ratio, chips = n_pt // n_tm, n_tm // 2
    devices = range(n_pt * n_tm)

    def permute(value, targets):
        return lax.ppermute(value, ("pt", "tm"), list(enumerate(targets)))

    def moved(n, places):
        sub = n // n_tm % ratio
        return n + ((sub + places) % ratio - sub) * n_tm

    mine = project(signals, freq_bins)
    other = permute(mine, [n ^ 1 for n in devices])
    chip_block = jnp.concatenate([mine, other], axis=0)
    blocks, origins = [], []
    for places, targets, passed in plan_rounds(chips, ratio):
        if passed is None:
            blocks.append(permute(chip_block, targets))
            origins.append((places, [targets.index(n) for n in devices]))
        else:
            blocks.append(permute(blocks[passed], [moved(n, places) for n in devices]))
            before = origins[passed][1]
            origins.append((places, [before[moved(n, -places)] for n in devices]))
    blocks.append(chip_block)
    origins.append((None, list(devices)))
    blocks, origins = blocks[::-1], origins[::-1]
    segments = samples // HALF * n_tm - 1
    scale = 1.0 / (segments * 0.375 * SEGLEN)
    rows = mine.shape[0]
    return pl.pallas_call(
        functools.partial(tiles_kernel, origins, chips, ratio, scale),
        out_shape=jax.ShapeDtypeStruct((2, NFREQ, points, ratio * points), jnp.float32),
        in_specs=[pl.BlockSpec(memory_space=pltpu.VMEM)] * len(blocks),
        out_specs=pl.BlockSpec(memory_space=pltpu.VMEM),
        scratch_shapes=[
            pltpu.VMEM((chips, 2, rows, LANES), jnp.float32),
            pltpu.VMEM((ratio, chips, 2, rows, LANES), jnp.float32),
        ],
        compiler_params=pltpu.CompilerParams(vmem_limit_bytes=VMEM_LIMIT),
        name="tiles",
    )(*blocks)


def solution(mesh):
    in_specs = (P("pt", "tm"), P())
    out_specs = P(None, None, "pt", "tm")
    return jax.shard_map(body, mesh=mesh, in_specs=in_specs, out_specs=out_specs, check_vma=False)
```

```python
import functools
import math

import jax
import jax.numpy as jnp
from jax import lax
from jax.experimental import pallas as pl
from jax.experimental.pallas import tpu as pltpu
from jax.sharding import PartitionSpec as P

SEGLEN = 1024
HALF = SEGLEN // 2
NFREQ = 4
COLS = 2 * NFREQ
LANES = 128
VMEM_LIMIT = 16 << 20
SERIES = [(-1) ** n / math.factorial(2 * n) for n in range(8)]
CONTRACT_LAST = (((1,), (1,)), ((), ()))
CONTRACT_FIRST = (((0,), (0,)), ((), ()))


TUNED_ROUNDS = (
    (0, (
        ((3, 1, 0, 2), (3, 1, 0, 2)),
        ((2, 3, 1, 0), (2, 3, 1, 0)),
        ((3, 0, 1, 2), (0, 3, 1, 2)),
        ((0, 3, 2, 1), (3, 2, 1, 0)),
    )),
    (1, 0),
    (1, (
        ((2, 0, 1, 3), (0, 2, 1, 3)),
        ((0, 1, 2, 3), (1, 0, 3, 2)),
        ((1, 2, 3, 0), (2, 1, 3, 0)),
        ((2, 1, 0, 3), (1, 0, 3, 2)),
    )),
    (0, (
        ((2, 0, 1, 3), (2, 0, 1, 3)),
        ((1, 0, 2, 3), (1, 0, 2, 3)),
        ((2, 1, 0, 3), (2, 1, 0, 3)),
        ((2, 1, 3, 0), (1, 0, 3, 2)),
    )),
    (None, 1),
)


def cosine_of(steps):
    wrapped = ((steps + HALF) & (SEGLEN - 1)) - HALF
    size = jnp.abs(wrapped)
    folded = size > HALF // 2
    size = jnp.where(folded, HALF - size, size)
    angle = size.astype(jnp.float32) * (2.0 * math.pi / SEGLEN)
    square = angle * angle
    value = jnp.full_like(square, SERIES[-1])
    for term in SERIES[-2::-1]:
        value = value * square + term
    return jnp.where(folded, -value, value)


def split(value):
    high = value.astype(jnp.bfloat16)
    low = (value - high.astype(jnp.float32)).astype(jnp.bfloat16)
    return high, low


def project_kernel(bins_hbm, signals_ref, out_ref, held, sems, bins_ref, bins_sem):
    pairs, width, _ = held.shape
    points = width // 2
    bins_copy = pltpu.make_async_copy(bins_hbm, bins_ref, bins_sem)
    bins_copy.start()
    copies = []
    for j in range(pairs):
        for h in range(2):
            copies.append(
                pltpu.make_async_copy(
                    signals_ref.at[:, pl.ds((j + pairs * h) * HALF, HALF)],
                    held.at[j, pl.ds(h * points, points), :],
                    sems.at[j, h],
                )
            )
            copies[-1].start()
    row = lax.broadcasted_iota(jnp.int32, (COLS, SEGLEN), 0)
    sample = lax.broadcasted_iota(jnp.int32, (COLS, SEGLEN), 1)
    window = 0.5 - 0.5 * cosine_of(sample)
    bins_copy.wait()
    bins = jnp.zeros((COLS, SEGLEN), jnp.int32)
    for f in range(NFREQ):
        bins = jnp.where(row % NFREQ == f, bins_ref[f], bins)
    quarter = jnp.where(row >= NFREQ, SEGLEN // 4, 0)
    table = window * cosine_of(sample * bins + quarter)
    high, low = split(jnp.concatenate([table[:, :HALF], table[:, HALF:]], axis=0))
    both = jnp.concatenate([high, low], axis=0)
    first, second = [], []
    step = 4 if pairs % 4 == 0 else 1
    for j in range(0, pairs, step):
        for copy in copies[2 * j : 2 * (j + step)]:
            copy.wait()
        block = jnp.concatenate([held[j + q] for q in range(step)], axis=0)
        block_high, block_low = split(block)
        main = lax.dot_general(both, block_high, CONTRACT_LAST, preferred_element_type=jnp.float32)
        rest = lax.dot_general(high, block_low, CONTRACT_LAST, preferred_element_type=jnp.float32)
        sums = main[: 2 * COLS] + main[2 * COLS :] + rest
        for q in range(step):
            first.append(sums[:COLS, q * width : (q + 1) * width])
            second.append(sums[COLS:, q * width : (q + 1) * width])
    for j in range(pairs - 1):
        out_ref[j * COLS : (j + 1) * COLS, :] = first[j] + second[j + 1]
    lane = lax.broadcasted_iota(jnp.int32, (COLS, width), 1)
    wrap = jnp.where(lane < points, pltpu.roll(second[0], points, 1), 0.0)
    out_ref[(pairs - 1) * COLS : pairs * COLS, :] = first[pairs - 1] + wrap
    out_ref[pairs * COLS :, :] = second[0]


def in_hbm(value):
    return pltpu.with_memory_space_constraint(value, pltpu.HBM)


def project(signals, freq_bins):
    points, samples = signals.shape
    pairs = samples // HALF // 2
    return pl.pallas_call(
        project_kernel,
        out_shape=jax.ShapeDtypeStruct(((pairs + 1) * COLS, 2 * points), jnp.float32),
        in_specs=[pl.BlockSpec(memory_space=pltpu.HBM)] * 2,
        out_specs=pl.BlockSpec(memory_space=pltpu.VMEM),
        scratch_shapes=[
            pltpu.VMEM((pairs, 2 * points, HALF), jnp.float32),
            pltpu.SemaphoreType.DMA((pairs, 2)),
            pltpu.SMEM((NFREQ,), jnp.int32),
            pltpu.SemaphoreType.DMA,
        ],
        compiler_params=pltpu.CompilerParams(vmem_limit_bytes=VMEM_LIMIT),
        name="project",
    )(in_hbm(freq_bins), in_hbm(signals))


def lookup(values, device):
    total = 0
    for bit in range(max(values).bit_length()):
        word = 0
        for start in range(0, len(values), 32):
            packed = sum((v >> bit & 1) << n for n, v in enumerate(values[start : start + 32]))
            packed -= (packed >> 31) << 32
            here = jnp.int32(packed)
            word = here if start == 0 else jnp.where(device >= start, here, word)
        total += (lax.shift_right_logical(word, lax.rem(device, 32)) & 1) << bit
    return total


def tiles_kernel(origins, chips, ratio, scale, *refs):
    blocks = refs[: len(origins)]
    out_ref, left, right = refs[len(origins) :]
    pt, tm = lax.axis_index("pt"), lax.axis_index("tm")
    device = pt * lax.axis_size("tm") + tm
    sub = lax.rem(pt, ratio)
    rows = left.shape[2]
    pairs = rows // COLS - 1
    points = LANES // 2

    for (places, sources), ref in zip(origins, blocks, strict=True):
        core = lookup([source % 2 for source in sources], device)
        chip = lookup([source // 2 % chips for source in sources], device)
        if places is None:
            dst = left.at[chip]
        else:
            dst = right.at[lax.rem(sub + ratio - places, ratio), chip]
        for c in range(2):
            dst[lax.rem(core + c, 2)] = ref[c * rows : (c + 1) * rows, :]

    lane = lax.broadcasted_iota(jnp.int32, (pairs, LANES), 1)
    low_half = lane < points
    last_row = (pairs - 1) * COLS
    low_lanes = lax.broadcasted_iota(jnp.int32, (COLS, LANES), 1) < points

    def finish(at):
        for t in range(2 * chips):
            here = at(t)
            value = here[last_row : last_row + COLS, :]
            if t + 1 < 2 * chips:
                extra = pltpu.roll(at(t + 1)[pairs * COLS :, :], points, 1)
                value = jnp.where(low_lanes, value, value + extra)
            else:
                value = jnp.where(low_lanes, value, 0.0)
            here[last_row : last_row + COLS, :] = value

    finish(lambda t: left.at[t // 2, t % 2])
    for b in range(ratio):
        finish(lambda t, b=b: right.at[b, t // 2, t % 2])

    def join(low, high):
        return (
            jnp.where(low_half, low, pltpu.roll(high, points, 1)),
            jnp.where(low_half, pltpu.roll(low, points, 1), high),
        )

    for f in range(NFREQ):
        lhs, rhs = [[], []], [[], []]
        for t in range(2 * chips):
            real, imag = (left.at[t // 2, t % 2][pl.ds(part * NFREQ + f, pairs, stride=COLS), :] for part in range(2))
            lhs[0] += join(real, imag)
            lhs[1] += join(imag, -real)
            for part in range(2):
                pick = pl.ds(part * NFREQ + f, pairs, stride=COLS)
                rhs[part] += join(*(right.at[b, t // 2, t % 2][pick, :] for b in range(2)))
        lhs_high, lhs_low = split(jnp.concatenate(lhs[0] + lhs[1], axis=0))
        rhs_high, rhs_low = split(jnp.concatenate(rhs[0] + rhs[1], axis=0))
        dot = functools.partial(
            lax.dot_general, dimension_numbers=CONTRACT_FIRST, preferred_element_type=jnp.float32
        )
        tile = dot(
            jnp.concatenate([lhs_high, lhs_high, lhs_low], axis=0),
            jnp.concatenate([rhs_high, rhs_low, rhs_high], axis=0),
        )
        tile = tile * scale
        out_ref[0, f] = tile[:points]
        out_ref[1, f] = tile[points:]


def plan_rounds(chips, ratio):
    cores = 2 * chips
    devices = [
        (group, sub, chip, core)
        for group in range(cores)
        for sub in range(ratio)
        for chip in range(chips)
        for core in range(2)
    ]
    number = {place: n for n, place in enumerate(devices)}

    def column(places, groups):
        targets = [
            number[groups[g][s][2 * x + c], (s + places) % ratio, g // 2, g % 2] for g, s, x, c in devices
        ]
        return places, targets, None

    def row(shift):
        return None, [number[g, s, (x + shift) % chips, c] for g, s, x, c in devices], None

    if (chips, ratio) == (2, 2):
        return [
            row(what) if places is None
            else (places, None, what) if isinstance(what, int)
            else column(places, what)
            for places, what in TUNED_ROUNDS
        ]
    rounds = []
    for m in range(chips):
        order = [2 * ((x + m) % chips) + c for x in range(chips) for c in range(2)]
        rounds.append(column(0, [[order] * ratio] * cores))
    rounds += [row(shift) for shift in range(1, chips)]
    for places in range(1, ratio):
        rounds += [(places, None, m) for m in range(chips)]
    return rounds


def body(signals, freq_bins):
    points, samples = signals.shape
    n_pt, n_tm = lax.axis_size("pt"), lax.axis_size("tm")
    ratio, chips = n_pt // n_tm, n_tm // 2
    devices = range(n_pt * n_tm)

    def permute(value, targets):
        return lax.ppermute(value, ("pt", "tm"), list(enumerate(targets)))

    def moved(n, places):
        sub = n // n_tm % ratio
        return n + ((sub + places) % ratio - sub) * n_tm

    mine = project(signals, freq_bins)
    other = permute(mine, [n ^ 1 for n in devices])
    chip_block = jnp.concatenate([mine, other], axis=0)
    blocks, origins = [], []
    for places, targets, passed in plan_rounds(chips, ratio):
        if passed is None:
            blocks.append(permute(chip_block, targets))
            origins.append((places, [targets.index(n) for n in devices]))
        else:
            blocks.append(permute(blocks[passed], [moved(n, places) for n in devices]))
            before = origins[passed][1]
            origins.append((places, [before[moved(n, -places)] for n in devices]))
    blocks.append(chip_block)
    origins.append((None, list(devices)))
    blocks, origins = blocks[::-1], origins[::-1]
    segments = samples // HALF * n_tm - 1
    scale = 1.0 / (segments * 0.375 * SEGLEN)
    rows = mine.shape[0]
    return pl.pallas_call(
        functools.partial(tiles_kernel, origins, chips, ratio, scale),
        out_shape=jax.ShapeDtypeStruct((2, NFREQ, points, ratio * points), jnp.float32),
        in_specs=[pl.BlockSpec(memory_space=pltpu.VMEM)] * len(blocks),
        out_specs=pl.BlockSpec(memory_space=pltpu.VMEM),
        scratch_shapes=[
            pltpu.VMEM((chips, 2, rows, LANES), jnp.float32),
            pltpu.VMEM((ratio, chips, 2, rows, LANES), jnp.float32),
        ],
        compiler_params=pltpu.CompilerParams(vmem_limit_bytes=VMEM_LIMIT),
        name="tiles",
    )(*blocks)


def solution(mesh):
    in_specs = (P("pt", "tm"), P())
    out_specs = P(None, None, "pt", "tm")
    return jax.shard_map(body, mesh=mesh, in_specs=in_specs, out_specs=out_specs, check_vma=False)
```
